32 devices in a mesh: ab: 4 (over y, x), cd: 4 (over z), ij: 2 (over core).
Axes of the slice: x: 2, y: 2, z: 4, core: 2. Of those that a mesh axis runs over, the one named last changes fastest.
Arguments:
- amplitudes: float32 [512, 4096], P('ij', ('cd', 'ab')), may hold values from -6 to 6
- integrals: float32 [256, 256, 256], P(('ab', 'cd')), may hold values from -0.375 to 0.375
- tile_row: int32 [256], P(('ab', 'cd')), may hold values from 0 to 3, as said below
- tile_col: int32 [256], P(('ab', 'cd')), may hold values from 0 to 3
- tile_count: int32 [16], P(('ab', 'cd')), may hold values from 1 to 16, as said below
Outputs:
- residual: float32 [512, 4, 16, 64], P('ij', 'ab', 'cd')
The draws below stay inside these ranges and needn't reach their ends.
Inputs may be any that keep to these rules, and one draw needn't show every extreme that they name: Within one slab the 16 slots name distinct (tile_row, tile_col) pairs. `tile_count`: in every draw some slab has all 16 slots live.
All inputs are finite; a program needn't handle non-finite values.
Results may differ from the reference program's by a relative error of at most 0.0003.
Values sent between devices are 32-bit elements; how exact they have to be, the bound alone decides.
A program may use at most 128 MiB of HBM per device.

```python
import jax
import jax.numpy as jnp
from jax import lax

OCC_DEV = 256
BS = 16
TS = 256
NBS = 4
OCC = 512
CT_DEV = 4
KT = 16
SLABS = 16
N_AB = 4
N_CD = 4


def tile_pairs(key):
    keys = jax.random.split(jax.random.fold_in(key, 11), SLABS)
    chosen = jax.vmap(lambda one_key: jax.random.permutation(one_key, NBS * CT_DEV)[:KT])(keys)
    return chosen.reshape(-1).astype(jnp.int32)


def draw_tile_row(key, part):
    return (tile_pairs(key) // CT_DEV).astype(jnp.int32)


def draw_tile_col(key, part):
    return (tile_pairs(key) % CT_DEV).astype(jnp.int32)


def draw_tile_count(key, part):
    counts = jax.random.randint(jax.random.fold_in(key, 5), (SLABS,), 1, KT + 1)
    fullest = jax.random.randint(jax.random.fold_in(key, 6), (), 0, SLABS)
    return counts.at[fullest].set(KT).astype(jnp.int32)


def level_of(rng, extent, pieces, smallest, high):
    level = 1.0
    for dim, shards_of in pieces:
        draws = jax.random.uniform(jax.random.fold_in(jax.random.fold_in(rng, 6), dim), (shards_of,), jnp.float32, smallest / len(pieces), high / len(pieces))
        level = level * jnp.repeat(jnp.exp(draws), extent[dim] // shards_of).reshape((-1,) + (1,) * (len(extent) - 1 - dim))
    return level


def gaussian(stream_key, shape, deviation, limit, cuts=(), kind=jnp.bfloat16):
    result = deviation * jax.random.normal(stream_key, shape, jnp.float32)
    if cuts:
        result = result * level_of(stream_key, shape, cuts, -0.22, 0.18)
    return jnp.clip(result, -limit, limit).astype(kind)


def setup_inputs(seed: int = 0) -> dict:
    key_of = jax.random.split(jax.random.key(seed), 6)
    amplitudes = gaussian(key_of[0], (OCC, N_AB * N_AB * TS), 1.0, 6.0, ((0, 2), (1, 16)), jnp.float32)
    integrals = gaussian(key_of[1], (SLABS * KT, TS, TS), TS ** -0.5, 0.375, ((0, 16),), jnp.float32)
    tile_row = draw_tile_row(jax.random.fold_in(key_of[5], 71), 0)
    tile_col = draw_tile_col(jax.random.fold_in(key_of[5], 71), 0)
    tile_count = draw_tile_count(jax.random.fold_in(key_of[5], 71), 0)
    return {"amplitudes": amplitudes, "integrals": integrals, "tile_row": tile_row, "tile_col": tile_col, "tile_count": tile_count}


def reference(amplitudes, integrals, tile_row, tile_col, tile_count):
    amp_tiles = amplitudes.reshape(OCC, N_AB * N_AB, TS)
    slab_tiles = integrals.reshape(SLABS, KT, TS, TS)
    slab_rows = tile_row.reshape(SLABS, KT)
    slab_cols = tile_col.reshape(SLABS, KT)
    slab_ids = jnp.arange(SLABS, dtype=jnp.int32)

    def add_slab(total, item):
        slab_id, tiles, rows, cols, live_count = item
        ab_index = slab_id // N_CD
        cd_index = slab_id % N_CD
        chosen = jnp.take(amp_tiles, (cd_index * CT_DEV + cols).astype(jnp.int32), axis=1)
        terms = jnp.einsum("okf,kef->oke", chosen, tiles, precision=lax.Precision.HIGHEST)
        live = (jnp.arange(KT, dtype=jnp.int32) < live_count).astype(jnp.float32)
        terms = terms * live[None, :, None]
        total = total.at[:, (ab_index * NBS + rows).astype(jnp.int32), :].add(terms)
        return total, None

    start = jnp.zeros((OCC, NBS * NBS, TS), jnp.float32)
    ladder, _ = lax.scan(add_slab, start, (slab_ids, slab_tiles, slab_rows, slab_cols, tile_count))
    ladder_five = ladder.reshape(OCC, NBS, NBS, BS, BS)
    partner = jnp.roll(ladder_five, OCC_DEV, axis=0)
    mirrored = jnp.transpose(partner, (0, 2, 1, 4, 3))
    total = ladder_five + mirrored
    return jnp.transpose(total, (0, 1, 3, 2, 4)).reshape(OCC, NBS, BS, NBS * BS)
```

```python
import functools
import math

import jax
import jax.numpy as jnp
from jax import lax
from jax.experimental import pallas as pl
from jax.experimental.pallas import tpu as pltpu
from jax.sharding import PartitionSpec as P

MESH = pl.DeviceIdType.MESH
LANES = 128


def split(value):
    high = value.astype(jnp.bfloat16)
    low = (value - high.astype(jnp.float32)).astype(jnp.bfloat16)
    return high, low


def ladder_kernel(
    n_ab, n_cd, block, chunks,
    row_ref, col_ref, count_ref, amp_ref, tiles_ref, out_ref,
    tiles, w_high, w_low, gathered, a_high, a_low, partial, arrived, summed, outgoing, mirrored,
    tile_sem, own_sem, ag_send, ag_recv, rs_send, rs_recv, mi_send, mi_recv,
):
    me_ab, me_cd, me_ij = lax.axis_index("ab"), lax.axis_index("cd"), lax.axis_index("ij")
    slots, size = tiles_ref.shape[0], tiles_ref.shape[1]
    group = block // n_cd
    rows = group * n_ab * block
    targets = n_ab * n_cd
    piece = group * group
    own_place = me_ab * n_cd + me_cd

    tile_copies = [
        pltpu.make_async_copy(tiles_ref.at[k], tiles.at[k], tile_sem.at[k]) for k in range(slots)
    ]
    for copy in tile_copies:
        copy.start()
    own = pltpu.make_async_copy(amp_ref, gathered.at[0], own_sem)
    own.start()

    barrier = pltpu.get_barrier_semaphore()
    for j in range(1, n_ab):
        pl.semaphore_signal(
            barrier, inc=1, device_id=(lax.rem(me_ab + j, n_ab), me_cd, me_ij), device_id_type=MESH
        )
    for i in range(1, n_cd):
        pl.semaphore_signal(
            barrier, inc=1, device_id=(me_ab, lax.rem(me_cd + i, n_cd), me_ij), device_id_type=MESH
        )
    for p in range(n_ab):
        for q in range(n_cd):
            pl.semaphore_signal(barrier, inc=1, device_id=(p, q, 1 - me_ij), device_id_type=MESH)
    pl.semaphore_wait(barrier, n_ab - 1 + n_cd - 1 + targets)

    ag = {}
    for h in range(chunks):
        part = pl.ds(h * LANES, LANES)
        for j in range(1, n_ab):
            ag[h, j] = pltpu.make_async_remote_copy(
                src_ref=amp_ref.at[part],
                dst_ref=gathered.at[j, part],
                send_sem=ag_send.at[h, j],
                recv_sem=ag_recv.at[h, j],
                device_id=(lax.rem(me_ab + j, n_ab), me_cd, me_ij),
                device_id_type=MESH,
            )
            ag[h, j].start()

    keys = [row_ref[k] * n_ab + col_ref[k] for k in range(slots)]
    live_count = count_ref[0]
    for copy in tile_copies:
        copy.wait()
    for j in range(n_ab):
        column = lax.rem(me_ab - j + n_ab, n_ab)
        for r in range(n_ab):
            slot = jnp.int32(0)
            for k in range(1, slots):
                slot = jnp.where(keys[k] == r * n_ab + column, jnp.int32(k), slot)
            scale = jnp.where(slot < live_count, jnp.float32(1), jnp.float32(0))
            high, low = split(tiles[slot] * scale)
            at = (slice(None), pl.ds(r * block, block), pl.ds(j * size, size))
            w_high[at] = high.reshape(block, block, size)
            w_low[at] = low.reshape(block, block, size)

    own.wait()
    rs = {}
    mi = {}
    contract = (((1,), (1,)), ((), ()))

    def finish(h):
        for i in range(1, n_cd):
            rs[h, i].wait_recv()
        total = partial[h, 0]
        for i in range(1, n_cd):
            total = total + arrived[h, i]
        summed[h] = total
        for x in range(group):
            for y in range(group):
                outgoing[h, pl.ds(x * group + y, targets, stride=piece), :] = summed[
                    h, pl.ds(x * n_ab * block + y, targets, stride=group), :
                ]
        for p in range(n_ab):
            for q in range(n_cd):
                t = p * n_cd + q
                mi[h, t] = pltpu.make_async_remote_copy(
                    src_ref=outgoing.at[h, pl.ds(t * piece, piece)],
                    dst_ref=mirrored.at[h, pl.ds(own_place * piece, piece)],
                    send_sem=mi_send.at[h, t],
                    recv_sem=mi_recv.at[h, own_place],
                    device_id=(p, q, 1 - me_ij),
                    device_id_type=MESH,
                )
                mi[h, t].start()

    for h in range(chunks):
        part = pl.ds(h * LANES, LANES)
        for j in range(n_ab):
            if j:
                ag[h, j].wait_recv()
            high, low = split(gathered[j, part])
            a_high[:, pl.ds(j * size, size)] = high
            a_low[:, pl.ds(j * size, size)] = low
        for i in [*range(1, n_cd), 0]:
            d = lax.rem(me_cd + i, n_cd)
            lead = pl.ds(d * group, group)
            left_high = w_high[lead].reshape(rows, n_ab * size)
            left_low = w_low[lead].reshape(rows, n_ab * size)
            right_high, right_low = a_high[...], a_low[...]
            value = lax.dot_general(
                left_high, right_low, contract, preferred_element_type=jnp.float32
            )
            value += lax.dot_general(
                left_low, right_high, contract, preferred_element_type=jnp.float32
            )
            value += lax.dot_general(
                left_high, right_high, contract, preferred_element_type=jnp.float32
            )
            partial[h, i] = value
            if i:
                rs[h, i] = pltpu.make_async_remote_copy(
                    src_ref=partial.at[h, i],
                    dst_ref=arrived.at[h, i],
                    send_sem=rs_send.at[h, i],
                    recv_sem=rs_recv.at[h, i],
                    device_id=(me_ab, d, me_ij),
                    device_id_type=MESH,
                )
                rs[h, i].start()
    for h in range(chunks):
        finish(h)
    for h in range(chunks):
        for s in range(targets):
            pltpu.make_async_remote_copy(
                src_ref=outgoing.at[h, pl.ds(s * piece, piece)],
                dst_ref=mirrored.at[h, pl.ds(s * piece, piece)],
                send_sem=mi_send.at[h, s],
                recv_sem=mi_recv.at[h, s],
                device_id=(me_ab, me_cd, 1 - me_ij),
                device_id_type=MESH,
            ).wait_recv()
        for y in range(group):
            out_ref[y, :, pl.ds(h * LANES, LANES)] = (
                summed[h, pl.ds(y * n_ab * block, n_ab * block), :]
                + mirrored[h, pl.ds(y, targets * group, stride=group), :]
            )
    for copy in [*ag.values(), *rs.values(), *mi.values()]:
        copy.wait_send()


def fused(amplitudes, integrals, tile_row, tile_col, tile_count):
    occ_dev = amplitudes.shape[0]
    slots, size = integrals.shape[0], integrals.shape[1]
    block = math.isqrt(size)
    n_ab, n_cd = lax.axis_size("ab"), lax.axis_size("cd")
    group = block // n_cd
    rows = group * n_ab * block
    chunks = occ_dev // LANES
    targets = n_ab * n_cd
    piece = group * group
    f32, bf16 = jnp.float32, jnp.bfloat16
    dma = pltpu.SemaphoreType.DMA
    out = pl.pallas_call(
        functools.partial(ladder_kernel, n_ab, n_cd, block, chunks),
        out_shape=jax.ShapeDtypeStruct((group, n_ab * block, occ_dev), f32),
        in_specs=[pl.BlockSpec(memory_space=pltpu.SMEM)] * 3
        + [pl.BlockSpec(memory_space=pl.ANY)] * 2,
        out_specs=pl.BlockSpec(memory_space=pltpu.VMEM),
        scratch_shapes=[
            pltpu.VMEM((slots, size, size), f32),
            pltpu.VMEM((block, n_ab * block, n_ab * size), bf16),
            pltpu.VMEM((block, n_ab * block, n_ab * size), bf16),
            pltpu.VMEM((n_ab, occ_dev, size), f32),
            pltpu.VMEM((LANES, n_ab * size), bf16),
            pltpu.VMEM((LANES, n_ab * size), bf16),
            pltpu.VMEM((chunks, n_cd, rows, LANES), f32),
            pltpu.VMEM((chunks, n_cd, rows, LANES), f32),
            pltpu.VMEM((chunks, rows, LANES), f32),
            pltpu.VMEM((chunks, targets * piece, LANES), f32),
            pltpu.VMEM((chunks, targets * piece, LANES), f32),
            dma((slots,)),
            dma,
            dma((chunks, n_ab)),
            dma((chunks, n_ab)),
            dma((chunks, n_cd)),
            dma((chunks, n_cd)),
            dma((chunks, targets)),
            dma((chunks, targets)),
        ],
        compiler_params=pltpu.CompilerParams(
            collective_id=0, has_side_effects=True, vmem_limit_bytes=48 * 1024 * 1024
        ),
    )(tile_row, tile_col, tile_count, amplitudes, integrals)
    return jnp.transpose(out, (2, 0, 1))[:, None]


def from_partner(block, axis, bit):
    count = lax.axis_size(axis)
    route = []
    for low in range(count):
        high = low | 1 << bit
        if high != low and high < count:
            route += [(low, high), (high, low)]
    return lax.ppermute(block, axis, route)


def place_rows(chosen, tile_rows, row_picks, block_size):
    terms = jnp.einsum("okf,kef->oke", chosen, tile_rows, precision=lax.Precision.HIGHEST)
    occ_dev, slots, width = terms.shape
    terms = terms.reshape(occ_dev, slots, width // block_size, block_size)
    placed = jnp.einsum("rk,okab->aorb", row_picks, terms, precision=lax.Precision.HIGHEST)
    return placed.reshape(width // block_size, occ_dev, row_picks.shape[0] * block_size)


def general(amplitudes, integrals, tile_row, tile_col, tile_count):
    occ_dev = amplitudes.shape[0]
    slots = integrals.shape[0]
    tile_size = integrals.shape[1]
    block_size = math.isqrt(tile_size)
    blocks = lax.axis_size("ab")
    cd_size = lax.axis_size("cd")
    group_size = block_size // cd_size
    live_count = tile_count[0]
    live = jnp.arange(slots, dtype=jnp.int32) < live_count
    row_picks = (
        (tile_row[None, :] == jnp.arange(blocks, dtype=jnp.int32)[:, None]) & live[None, :]
    ).astype(jnp.float32)
    gathered = lax.all_gather(amplitudes, "ab", axis=1, tiled=True)
    columns = gathered.reshape(occ_dev, -1, tile_size)
    chosen = jnp.take(columns, tile_col, axis=1)
    partial_value = place_rows(chosen, integrals, row_picks, block_size)
    summed = lax.psum_scatter(partial_value, "cd", scatter_dimension=0, tiled=True)
    direct = jnp.transpose(summed, (1, 0, 2))
    outgoing = summed.reshape(group_size, occ_dev, blocks, cd_size, group_size)
    outgoing = jnp.transpose(outgoing, (2, 3, 1, 0, 4))
    arrived = lax.all_to_all(
        outgoing.reshape(blocks * cd_size, occ_dev * group_size * group_size),
        ("ab", "cd"),
        split_axis=0,
        concat_axis=0,
        tiled=True,
    )
    arrived = arrived.reshape(blocks, cd_size, occ_dev, group_size, group_size)
    mirrored = jnp.transpose(arrived, (2, 4, 0, 1, 3)).reshape(
        occ_dev, group_size, blocks * block_size
    )
    partner = from_partner(mirrored, "ij", 0)
    return (direct + partner).reshape(occ_dev, 1, group_size, blocks * block_size)


def per_device(amplitudes, integrals, tile_row, tile_col, tile_count):
    n_ab = lax.axis_size("ab")
    if (
        amplitudes.shape[1] == integrals.shape[1]
        and integrals.shape[0] == n_ab * n_ab
        and lax.axis_size("ij") == 2
        and amplitudes.shape[0] % LANES == 0
    ):
        return fused(amplitudes, integrals, tile_row, tile_col, tile_count)
    return general(amplitudes, integrals, tile_row, tile_col, tile_count)


def solution(mesh):
    in_specs = (
        P("ij", ("cd", "ab")),
        P(("ab", "cd"), None, None),
        P(("ab", "cd")),
        P(("ab", "cd")),
        P(("ab", "cd")),
    )
    out_specs = P("ij", "ab", "cd", None)
    return jax.shard_map(
        per_device, mesh=mesh, in_specs=in_specs, out_specs=out_specs, check_vma=False
    )
```

```python
import functools
import math

import jax
import jax.numpy as jnp
from jax import lax
from jax.experimental import pallas as pl
from jax.experimental.pallas import tpu as pltpu
from jax.sharding import PartitionSpec as P

MESH = pl.DeviceIdType.MESH
LANES = 128
VMEM_BYTES = 63 * 1024 * 1024


def split(value):
    high = value.astype(jnp.bfloat16)
    low = (value - high.astype(jnp.float32)).astype(jnp.bfloat16)
    return high, low


def ladder_kernel(
    n_ab, n_cd, block, chunks,
    row_ref, col_ref, count_ref, amp_ref, tiles_ref, out_ref,
    tiles, w_high, w_low, gathered, a_high, a_low, partial, up_in, down_in, up_out, down_out,
    summed, outgoing, mirrored,
    tile_sem, own_sem, ag_send, ag_recv, up_send, up_recv, down_send, down_recv,
    mi_send, mi_recv,
):
    me_ab, me_cd, me_ij = lax.axis_index("ab"), lax.axis_index("cd"), lax.axis_index("ij")
    slots, size = tiles_ref.shape[0], tiles_ref.shape[1]
    group = block // n_cd
    rows = group * n_ab * block
    targets = n_ab * n_cd
    piece = group * group
    own_place = me_ab * n_cd + me_cd

    tile_copies = [
        pltpu.make_async_copy(tiles_ref.at[k], tiles.at[k], tile_sem.at[k]) for k in range(slots)
    ]
    for copy in tile_copies:
        copy.start()
    own = pltpu.make_async_copy(amp_ref, gathered.at[0], own_sem)
    own.start()

    barrier = pltpu.get_barrier_semaphore()
    for j in range(1, n_ab):
        pl.semaphore_signal(
            barrier, inc=1, device_id=(lax.rem(me_ab + j, n_ab), me_cd, me_ij), device_id_type=MESH
        )
    for i in range(1, n_cd):
        pl.semaphore_signal(
            barrier, inc=1, device_id=(me_ab, lax.rem(me_cd + i, n_cd), me_ij), device_id_type=MESH
        )
    for p in range(n_ab):
        for q in range(n_cd):
            pl.semaphore_signal(barrier, inc=1, device_id=(p, q, 1 - me_ij), device_id_type=MESH)
    pl.semaphore_wait(barrier, n_ab - 1 + n_cd - 1 + targets)

    ag = {}
    for h in range(chunks):
        part = pl.ds(h * LANES, LANES)
        for j in range(1, n_ab):
            ag[h, j] = pltpu.make_async_remote_copy(
                src_ref=amp_ref.at[part],
                dst_ref=gathered.at[j, part],
                send_sem=ag_send.at[h, j],
                recv_sem=ag_recv.at[h, j],
                device_id=(lax.rem(me_ab + j, n_ab), me_cd, me_ij),
                device_id_type=MESH,
            )
            ag[h, j].start()

    keys = [row_ref[k] * n_ab + col_ref[k] for k in range(slots)]
    live_count = count_ref[0]
    for copy in tile_copies:
        copy.wait()
    for j in range(n_ab):
        column = lax.rem(me_ab - j + n_ab, n_ab)
        for r in range(n_ab):
            slot = jnp.int32(0)
            for k in range(1, slots):
                slot = jnp.where(keys[k] == r * n_ab + column, jnp.int32(k), slot)
            scale = jnp.where(slot < live_count, jnp.float32(1), jnp.float32(0))
            high, low = split(tiles[slot] * scale)
            at = (slice(None), pl.ds(r * block, block), pl.ds(j * size, size))
            w_high[at] = high.reshape(block, block, size)
            w_low[at] = low.reshape(block, block, size)

    own.wait()
    mi = {}
    contract = (((1,), (1,)), ((), ()))
    last = n_cd - 1

    def up(h, d, source):
        return pltpu.make_async_remote_copy(
            src_ref=source.at[h, d],
            dst_ref=up_in.at[h, d],
            send_sem=up_send.at[h, d],
            recv_sem=up_recv.at[h, d],
            device_id=(me_ab, me_cd + 1, me_ij),
            device_id_type=MESH,
        )

    def down(h, d, source):
        return pltpu.make_async_remote_copy(
            src_ref=source.at[h, d],
            dst_ref=down_in.at[h, d],
            send_sem=down_send.at[h, d],
            recv_sem=down_recv.at[h, d],
            device_id=(me_ab, me_cd - 1, me_ij),
            device_id_type=MESH,
        )

    def compute(h):
        part = pl.ds(h * LANES, LANES)
        for j in range(n_ab):
            if j:
                ag[h, j].wait_recv()
            high, low = split(gathered[j, part])
            a_high[:, pl.ds(j * size, size)] = high
            a_low[:, pl.ds(j * size, size)] = low
        for i in range(n_cd):
            d = jnp.where(me_cd < n_cd // 2, last - i, i)
            lead = pl.ds(d * group, group)
            left_high = w_high[lead].reshape(rows, n_ab * size)
            left_low = w_low[lead].reshape(rows, n_ab * size)
            right_high, right_low = a_high[...], a_low[...]
            value = lax.dot_general(
                left_high, right_low, contract, preferred_element_type=jnp.float32
            )
            value += lax.dot_general(
                left_low, right_high, contract, preferred_element_type=jnp.float32
            )
            value += lax.dot_general(
                left_high, right_high, contract, preferred_element_type=jnp.float32
            )
            partial[h, d] = value
            if i < last:

                @pl.when(me_cd == 0)
                def _():
                    up(h, d, partial).start()

                @pl.when(me_cd == last)
                def _():
                    down(h, d, partial).start()

    def relay(h, step):
        for_up = last + me_cd - step

        @pl.when((me_cd >= 1) & (me_cd <= step))
        def _():
            up(h, for_up, up_out).wait_recv()
            if step < last:
                up_out[h, for_up] = partial[h, for_up] + up_in[h, for_up]
                up(h, for_up, up_out).start()

        for_down = step - last + me_cd

        @pl.when((me_cd < last) & (for_down >= 0))
        def _():
            down(h, for_down, down_out).wait_recv()
            if step < last:
                down_out[h, for_down] = partial[h, for_down] + down_in[h, for_down]
                down(h, for_down, down_out).start()

    def finish(h):
        summed[h] = partial[h, me_cd]

        @pl.when(me_cd > 0)
        def _():
            summed[h] += up_in[h, me_cd]

        @pl.when(me_cd < last)
        def _():
            summed[h] += down_in[h, me_cd]

        for x in range(group):
            for y in range(group):
                outgoing[h, pl.ds(x * group + y, targets, stride=piece), :] = summed[
                    h, pl.ds(x * n_ab * block + y, targets, stride=group), :
                ]
        for p in range(n_ab):
            for q in range(n_cd):
                t = p * n_cd + q
                mi[h, t] = pltpu.make_async_remote_copy(
                    src_ref=outgoing.at[h, pl.ds(t * piece, piece)],
                    dst_ref=mirrored.at[h, pl.ds(own_place * piece, piece)],
                    send_sem=mi_send.at[h, t],
                    recv_sem=mi_recv.at[h, own_place],
                    device_id=(p, q, 1 - me_ij),
                    device_id_type=MESH,
                )
                mi[h, t].start()

    waiting = None
    for h in range(chunks):
        compute(h)
        if waiting is not None:
            for step in range(2, n_cd):
                relay(waiting, step)
            finish(waiting)
        relay(h, 1)
        waiting = h
    for step in range(2, n_cd):
        relay(waiting, step)
    finish(waiting)
    for h in range(chunks):
        for s in range(targets):
            pltpu.make_async_remote_copy(
                src_ref=outgoing.at[h, pl.ds(s * piece, piece)],
                dst_ref=mirrored.at[h, pl.ds(s * piece, piece)],
                send_sem=mi_send.at[h, s],
                recv_sem=mi_recv.at[h, s],
                device_id=(me_ab, me_cd, 1 - me_ij),
                device_id_type=MESH,
            ).wait_recv()
        for y in range(group):
            out_ref[y, :, pl.ds(h * LANES, LANES)] = (
                summed[h, pl.ds(y * n_ab * block, n_ab * block), :]
                + mirrored[h, pl.ds(y, targets * group, stride=group), :]
            )
    for h in range(chunks):
        for d in range(n_cd):

            @pl.when(me_cd < d)
            def _():
                up(h, d, up_out).wait_send()

            @pl.when(me_cd > d)
            def _():
                down(h, d, down_out).wait_send()

    for copy in [*ag.values(), *mi.values()]:
        copy.wait_send()


def fused(amplitudes, integrals, tile_row, tile_col, tile_count):
    occ_dev = amplitudes.shape[0]
    slots, size = integrals.shape[0], integrals.shape[1]
    block = math.isqrt(size)
    n_ab, n_cd = lax.axis_size("ab"), lax.axis_size("cd")
    group = block // n_cd
    rows = group * n_ab * block
    chunks = occ_dev // LANES
    targets = n_ab * n_cd
    piece = group * group
    f32, bf16 = jnp.float32, jnp.bfloat16
    dma = pltpu.SemaphoreType.DMA
    out = pl.pallas_call(
        functools.partial(ladder_kernel, n_ab, n_cd, block, chunks),
        out_shape=jax.ShapeDtypeStruct((group, n_ab * block, occ_dev), f32),
        in_specs=[pl.BlockSpec(memory_space=pltpu.SMEM)] * 3
        + [pl.BlockSpec(memory_space=pl.ANY)] * 2,
        out_specs=pl.BlockSpec(memory_space=pltpu.VMEM),
        scratch_shapes=[
            pltpu.VMEM((slots, size, size), f32),
            pltpu.VMEM((block, n_ab * block, n_ab * size), bf16),
            pltpu.VMEM((block, n_ab * block, n_ab * size), bf16),
            pltpu.VMEM((n_ab, occ_dev, size), f32),
            pltpu.VMEM((LANES, n_ab * size), bf16),
            pltpu.VMEM((LANES, n_ab * size), bf16),
            *[pltpu.VMEM((chunks, n_cd, rows, LANES), f32)] * 5,
            pltpu.VMEM((chunks, rows, LANES), f32),
            pltpu.VMEM((chunks, targets * piece, LANES), f32),
            pltpu.VMEM((chunks, targets * piece, LANES), f32),
            dma((slots,)),
            dma,
            dma((chunks, n_ab)),
            dma((chunks, n_ab)),
            *[dma((chunks, n_cd))] * 4,
            dma((chunks, targets)),
            dma((chunks, targets)),
        ],
        compiler_params=pltpu.CompilerParams(
            collective_id=0, has_side_effects=True, vmem_limit_bytes=VMEM_BYTES
        ),
    )(tile_row, tile_col, tile_count, amplitudes, integrals)
    return jnp.transpose(out, (2, 0, 1))[:, None]


def from_partner(block, axis, bit):
    count = lax.axis_size(axis)
    route = []
    for low in range(count):
        high = low | 1 << bit
        if high != low and high < count:
            route += [(low, high), (high, low)]
    return lax.ppermute(block, axis, route)


def place_rows(chosen, tile_rows, row_picks, block_size):
    terms = jnp.einsum("okf,kef->oke", chosen, tile_rows, precision=lax.Precision.HIGHEST)
    occ_dev, slots, width = terms.shape
    terms = terms.reshape(occ_dev, slots, width // block_size, block_size)
    placed = jnp.einsum("rk,okab->aorb", row_picks, terms, precision=lax.Precision.HIGHEST)
    return placed.reshape(width // block_size, occ_dev, row_picks.shape[0] * block_size)


def general(amplitudes, integrals, tile_row, tile_col, tile_count):
    occ_dev = amplitudes.shape[0]
    slots = integrals.shape[0]
    tile_size = integrals.shape[1]
    block_size = math.isqrt(tile_size)
    blocks = lax.axis_size("ab")
    cd_size = lax.axis_size("cd")
    group_size = block_size // cd_size
    live_count = tile_count[0]
    live = jnp.arange(slots, dtype=jnp.int32) < live_count
    row_picks = (
        (tile_row[None, :] == jnp.arange(blocks, dtype=jnp.int32)[:, None]) & live[None, :]
    ).astype(jnp.float32)
    gathered = lax.all_gather(amplitudes, "ab", axis=1, tiled=True)
    columns = gathered.reshape(occ_dev, -1, tile_size)
    chosen = jnp.take(columns, tile_col, axis=1)
    partial_value = place_rows(chosen, integrals, row_picks, block_size)
    summed = lax.psum_scatter(partial_value, "cd", scatter_dimension=0, tiled=True)
    direct = jnp.transpose(summed, (1, 0, 2))
    outgoing = summed.reshape(group_size, occ_dev, blocks, cd_size, group_size)
    outgoing = jnp.transpose(outgoing, (2, 3, 1, 0, 4))
    arrived = lax.all_to_all(
        outgoing.reshape(blocks * cd_size, occ_dev * group_size * group_size),
        ("ab", "cd"),
        split_axis=0,
        concat_axis=0,
        tiled=True,
    )
    arrived = arrived.reshape(blocks, cd_size, occ_dev, group_size, group_size)
    mirrored = jnp.transpose(arrived, (2, 4, 0, 1, 3)).reshape(
        occ_dev, group_size, blocks * block_size
    )
    partner = from_partner(mirrored, "ij", 0)
    return (direct + partner).reshape(occ_dev, 1, group_size, blocks * block_size)


def per_device(amplitudes, integrals, tile_row, tile_col, tile_count):
    n_ab = lax.axis_size("ab")
    if (
        amplitudes.shape[1] == integrals.shape[1]
        and integrals.shape[0] == n_ab * n_ab
        and lax.axis_size("ij") == 2
        and amplitudes.shape[0] % LANES == 0
    ):
        return fused(amplitudes, integrals, tile_row, tile_col, tile_count)
    return general(amplitudes, integrals, tile_row, tile_col, tile_count)


def solution(mesh):
    in_specs = (
        P("ij", ("cd", "ab")),
        P(("ab", "cd"), None, None),
        P(("ab", "cd")),
        P(("ab", "cd")),
        P(("ab", "cd")),
    )
    out_specs = P("ij", "ab", "cd", None)
    return jax.shard_map(
        per_device, mesh=mesh, in_specs=in_specs, out_specs=out_specs, check_vma=False
    )
```

```python
import functools
import math

import jax
import jax.numpy as jnp
from jax import lax
from jax.experimental import pallas as pl
from jax.experimental.pallas import tpu as pltpu
from jax.sharding import PartitionSpec as P

MESH = pl.DeviceIdType.MESH
LANES = 128
VMEM_BYTES = 63 * 1024 * 1024


def split(value):
    high = value.astype(jnp.bfloat16)
    low = (value - high.astype(jnp.float32)).astype(jnp.bfloat16)
    return high, low


def ladder_kernel(
    n_ab, n_cd, block, chunks,
    row_ref, col_ref, count_ref, amp_ref, tiles_ref, out_ref,
    tiles, w_high, w_low, gathered, a_high, a_low, partial, up_in, down_in, up_out, down_out,
    summed, outgoing, mirrored,
    tile_sem, own_sem, ag_send, ag_recv, up_send, up_recv, down_send, down_recv,
    mi_send, mi_recv,
):
    me_ab, me_cd, me_ij = lax.axis_index("ab"), lax.axis_index("cd"), lax.axis_index("ij")
    slots, size = tiles_ref.shape[0], tiles_ref.shape[1]
    group = block // n_cd
    rows = group * n_ab * block
    targets = n_ab * n_cd
    piece = group * group
    own_place = me_ab * n_cd + me_cd

    tile_copies = [
        pltpu.make_async_copy(tiles_ref.at[k], tiles.at[k], tile_sem.at[k]) for k in range(slots)
    ]
    for copy in tile_copies:
        copy.start()
    own = pltpu.make_async_copy(amp_ref, gathered.at[0], own_sem)
    own.start()

    barrier = pltpu.get_barrier_semaphore()
    for j in range(1, n_ab):
        pl.semaphore_signal(
            barrier, inc=1, device_id=(lax.rem(me_ab + j, n_ab), me_cd, me_ij), device_id_type=MESH
        )
    pl.semaphore_signal(barrier, inc=1, device_id=(me_ab, me_cd, 1 - me_ij), device_id_type=MESH)

    @pl.when(me_cd > 0)
    def _():
        pl.semaphore_signal(barrier, inc=1, device_id=(me_ab, me_cd - 1, me_ij), device_id_type=MESH)

    @pl.when(me_cd < n_cd - 1)
    def _():
        pl.semaphore_signal(barrier, inc=1, device_id=(me_ab, me_cd + 1, me_ij), device_id_type=MESH)

    ends = jnp.where(me_cd > 0, 1, 0) + jnp.where(me_cd < n_cd - 1, 1, 0)
    pl.semaphore_wait(barrier, n_ab + ends)

    ag = {}
    for h in range(chunks):
        part = pl.ds(h * LANES, LANES)
        for j in range(1, n_ab):
            ag[h, j] = pltpu.make_async_remote_copy(
                src_ref=amp_ref.at[part],
                dst_ref=gathered.at[j, part],
                send_sem=ag_send.at[h, j],
                recv_sem=ag_recv.at[h, j],
                device_id=(lax.rem(me_ab + j, n_ab), me_cd, me_ij),
                device_id_type=MESH,
            )
            ag[h, j].start()

    keys = [row_ref[k] * n_ab + col_ref[k] for k in range(slots)]
    live_count = count_ref[0]
    for copy in tile_copies:
        copy.wait()
    for j in range(n_ab):
        column = lax.rem(me_ab - j + n_ab, n_ab)
        for r in range(n_ab):
            slot = jnp.int32(0)
            for k in range(1, slots):
                slot = jnp.where(keys[k] == r * n_ab + column, jnp.int32(k), slot)
            scale = jnp.where(slot < live_count, jnp.float32(1), jnp.float32(0))
            high, low = split(tiles[slot] * scale)
            at = (slice(None), pl.ds(r * block, block), pl.ds(j * size, size))
            w_high[at] = high.reshape(block, block, size)
            w_low[at] = low.reshape(block, block, size)

    own.wait()
    mi = {}
    contract = (((1,), (1,)), ((), ()))
    last = n_cd - 1

    def up(h, d, source):
        return pltpu.make_async_remote_copy(
            src_ref=source.at[h, d],
            dst_ref=up_in.at[h, d],
            send_sem=up_send.at[h, d],
            recv_sem=up_recv.at[h, d],
            device_id=(me_ab, me_cd + 1, me_ij),
            device_id_type=MESH,
        )

    def down(h, d, source):
        return pltpu.make_async_remote_copy(
            src_ref=source.at[h, d],
            dst_ref=down_in.at[h, d],
            send_sem=down_send.at[h, d],
            recv_sem=down_recv.at[h, d],
            device_id=(me_ab, me_cd - 1, me_ij),
            device_id_type=MESH,
        )

    def compute(h):
        part = pl.ds(h * LANES, LANES)
        for j in range(n_ab):
            if j:
                ag[h, j].wait_recv()
            high, low = split(gathered[j, part])
            a_high[:, pl.ds(j * size, size)] = high
            a_low[:, pl.ds(j * size, size)] = low
        for i in range(n_cd):
            d = jnp.where(me_cd < n_cd // 2, last - i, i)
            lead = pl.ds(d * group, group)
            left_high = w_high[lead].reshape(rows, n_ab * size)
            left_low = w_low[lead].reshape(rows, n_ab * size)
            right_high, right_low = a_high[...], a_low[...]
            value = lax.dot_general(
                left_high, right_low, contract, preferred_element_type=jnp.float32
            )
            value += lax.dot_general(
                left_low, right_high, contract, preferred_element_type=jnp.float32
            )
            value += lax.dot_general(
                left_high, right_high, contract, preferred_element_type=jnp.float32
            )
            partial[h, d] = value
            if i < last:

                @pl.when(me_cd == 0)
                def _():
                    up(h, d, partial).start()

                @pl.when(me_cd == last)
                def _():
                    down(h, d, partial).start()

    def relay(h, step):
        for_up = last + me_cd - step

        @pl.when((me_cd >= 1) & (me_cd <= step))
        def _():
            up(h, for_up, up_out).wait_recv()
            if step < last:
                up_out[h, for_up] = partial[h, for_up] + up_in[h, for_up]
                up(h, for_up, up_out).start()

        for_down = step - last + me_cd

        @pl.when((me_cd < last) & (for_down >= 0))
        def _():
            down(h, for_down, down_out).wait_recv()
            if step < last:
                down_out[h, for_down] = partial[h, for_down] + down_in[h, for_down]
                down(h, for_down, down_out).start()

    def finish(h):
        summed[h] = partial[h, me_cd]

        @pl.when(me_cd > 0)
        def _():
            summed[h] += up_in[h, me_cd]

        @pl.when(me_cd < last)
        def _():
            summed[h] += down_in[h, me_cd]

        for x in range(group):
            for y in range(group):
                outgoing[h, pl.ds(x * group + y, targets, stride=piece), :] = summed[
                    h, pl.ds(x * n_ab * block + y, targets, stride=group), :
                ]
        for i in range(n_cd):
            q = jnp.where(me_cd < n_cd // 2, last - i, i)
            for j in range(n_ab):
                p = lax.rem(me_ab + j, n_ab)
                t = p * n_cd + q
                mi[h, i, j] = pltpu.make_async_remote_copy(
                    src_ref=outgoing.at[h, pl.ds(t * piece, piece)],
                    dst_ref=mirrored.at[h, pl.ds(own_place * piece, piece)],
                    send_sem=mi_send.at[h, t],
                    recv_sem=mi_recv.at[h, own_place],
                    device_id=(p, q, 1 - me_ij),
                    device_id_type=MESH,
                )
                mi[h, i, j].start()

    waiting = None
    for h in range(chunks):
        compute(h)
        if waiting is not None:
            for step in range(2, n_cd):
                relay(waiting, step)
            finish(waiting)
        relay(h, 1)
        waiting = h
    for step in range(2, n_cd):
        relay(waiting, step)
    finish(waiting)
    for h in range(chunks):
        for s in range(targets):
            pltpu.make_async_remote_copy(
                src_ref=outgoing.at[h, pl.ds(s * piece, piece)],
                dst_ref=mirrored.at[h, pl.ds(s * piece, piece)],
                send_sem=mi_send.at[h, s],
                recv_sem=mi_recv.at[h, s],
                device_id=(me_ab, me_cd, 1 - me_ij),
                device_id_type=MESH,
            ).wait_recv()
        for y in range(group):
            out_ref[y, :, pl.ds(h * LANES, LANES)] = (
                summed[h, pl.ds(y * n_ab * block, n_ab * block), :]
                + mirrored[h, pl.ds(y, targets * group, stride=group), :]
            )
    for h in range(chunks):
        for d in range(n_cd):

            @pl.when(me_cd < d)
            def _():
                up(h, d, up_out).wait_send()

            @pl.when(me_cd > d)
            def _():
                down(h, d, down_out).wait_send()

    for copy in [*ag.values(), *mi.values()]:
        copy.wait_send()


def fused(amplitudes, integrals, tile_row, tile_col, tile_count):
    occ_dev = amplitudes.shape[0]
    slots, size = integrals.shape[0], integrals.shape[1]
    block = math.isqrt(size)
    n_ab, n_cd = lax.axis_size("ab"), lax.axis_size("cd")
    group = block // n_cd
    rows = group * n_ab * block
    chunks = occ_dev // LANES
    targets = n_ab * n_cd
    piece = group * group
    f32, bf16 = jnp.float32, jnp.bfloat16
    dma = pltpu.SemaphoreType.DMA
    out = pl.pallas_call(
        functools.partial(ladder_kernel, n_ab, n_cd, block, chunks),
        out_shape=jax.ShapeDtypeStruct((group, n_ab * block, occ_dev), f32),
        in_specs=[pl.BlockSpec(memory_space=pltpu.SMEM)] * 3
        + [pl.BlockSpec(memory_space=pl.ANY)] * 2,
        out_specs=pl.BlockSpec(memory_space=pltpu.VMEM),
        scratch_shapes=[
            pltpu.VMEM((slots, size, size), f32),
            pltpu.VMEM((block, n_ab * block, n_ab * size), bf16),
            pltpu.VMEM((block, n_ab * block, n_ab * size), bf16),
            pltpu.VMEM((n_ab, occ_dev, size), f32),
            pltpu.VMEM((LANES, n_ab * size), bf16),
            pltpu.VMEM((LANES, n_ab * size), bf16),
            *[pltpu.VMEM((chunks, n_cd, rows, LANES), f32)] * 5,
            pltpu.VMEM((chunks, rows, LANES), f32),
            pltpu.VMEM((chunks, targets * piece, LANES), f32),
            pltpu.VMEM((chunks, targets * piece, LANES), f32),
            dma((slots,)),
            dma,
            dma((chunks, n_ab)),
            dma((chunks, n_ab)),
            *[dma((chunks, n_cd))] * 4,
            dma((chunks, targets)),
            dma((chunks, targets)),
        ],
        compiler_params=pltpu.CompilerParams(
            collective_id=0, has_side_effects=True, vmem_limit_bytes=VMEM_BYTES
        ),
    )(tile_row, tile_col, tile_count, amplitudes, integrals)
    return jnp.transpose(out, (2, 0, 1))[:, None]


def from_partner(block, axis, bit):
    count = lax.axis_size(axis)
    route = []
    for low in range(count):
        high = low | 1 << bit
        if high != low and high < count:
            route += [(low, high), (high, low)]
    return lax.ppermute(block, axis, route)


def place_rows(chosen, tile_rows, row_picks, block_size):
    terms = jnp.einsum("okf,kef->oke", chosen, tile_rows, precision=lax.Precision.HIGHEST)
    occ_dev, slots, width = terms.shape
    terms = terms.reshape(occ_dev, slots, width // block_size, block_size)
    placed = jnp.einsum("rk,okab->aorb", row_picks, terms, precision=lax.Precision.HIGHEST)
    return placed.reshape(width // block_size, occ_dev, row_picks.shape[0] * block_size)


def general(amplitudes, integrals, tile_row, tile_col, tile_count):
    occ_dev = amplitudes.shape[0]
    slots = integrals.shape[0]
    tile_size = integrals.shape[1]
    block_size = math.isqrt(tile_size)
    blocks = lax.axis_size("ab")
    cd_size = lax.axis_size("cd")
    group_size = block_size // cd_size
    live_count = tile_count[0]
    live = jnp.arange(slots, dtype=jnp.int32) < live_count
    row_picks = (
        (tile_row[None, :] == jnp.arange(blocks, dtype=jnp.int32)[:, None]) & live[None, :]
    ).astype(jnp.float32)
    gathered = lax.all_gather(amplitudes, "ab", axis=1, tiled=True)
    columns = gathered.reshape(occ_dev, -1, tile_size)
    chosen = jnp.take(columns, tile_col, axis=1)
    partial_value = place_rows(chosen, integrals, row_picks, block_size)
    summed = lax.psum_scatter(partial_value, "cd", scatter_dimension=0, tiled=True)
    direct = jnp.transpose(summed, (1, 0, 2))
    outgoing = summed.reshape(group_size, occ_dev, blocks, cd_size, group_size)
    outgoing = jnp.transpose(outgoing, (2, 3, 1, 0, 4))
    arrived = lax.all_to_all(
        outgoing.reshape(blocks * cd_size, occ_dev * group_size * group_size),
        ("ab", "cd"),
        split_axis=0,
        concat_axis=0,
        tiled=True,
    )
    arrived = arrived.reshape(blocks, cd_size, occ_dev, group_size, group_size)
    mirrored = jnp.transpose(arrived, (2, 4, 0, 1, 3)).reshape(
        occ_dev, group_size, blocks * block_size
    )
    partner = from_partner(mirrored, "ij", 0)
    return (direct + partner).reshape(occ_dev, 1, group_size, blocks * block_size)


def per_device(amplitudes, integrals, tile_row, tile_col, tile_count):
    n_ab = lax.axis_size("ab")
    if (
        amplitudes.shape[1] == integrals.shape[1]
        and integrals.shape[0] == n_ab * n_ab
        and lax.axis_size("ij") == 2
        and amplitudes.shape[0] % LANES == 0
    ):
        return fused(amplitudes, integrals, tile_row, tile_col, tile_count)
    return general(amplitudes, integrals, tile_row, tile_col, tile_count)


def solution(mesh):
    in_specs = (
        P("ij", ("cd", "ab")),
        P(("ab", "cd"), None, None),
        P(("ab", "cd")),
        P(("ab", "cd")),
        P(("ab", "cd")),
    )
    out_specs = P("ij", "ab", "cd", None)
    return jax.shard_map(
        per_device, mesh=mesh, in_specs=in_specs, out_specs=out_specs, check_vma=False
    )
```

```python
import functools
import math

import jax
import jax.numpy as jnp
from jax import lax
from jax.experimental import pallas as pl
from jax.experimental.pallas import tpu as pltpu
from jax.sharding import PartitionSpec as P

MESH = pl.DeviceIdType.MESH
LANES = 128
VMEM_BYTES = 63 * 1024 * 1024


def split(value):
    high = value.astype(jnp.bfloat16)
    low = (value - high.astype(jnp.float32)).astype(jnp.bfloat16)
    return high, low


def ladder_kernel(
    n_ab, n_cd, block, chunks,
    row_ref, col_ref, count_ref, amp_ref, tiles_ref, out_ref,
    tiles, w_high, w_low, gathered, a_both, partial, up_in, down_in, up_out, down_out,
    summed, outgoing, mirrored,
    tile_sem, own_sem, ag_send, ag_recv, up_send, up_recv, down_send, down_recv,
    mi_send, mi_recv,
):
    me_ab, me_cd, me_ij = lax.axis_index("ab"), lax.axis_index("cd"), lax.axis_index("ij")
    slots, size = tiles_ref.shape[0], tiles_ref.shape[1]
    group = block // n_cd
    rows = group * n_ab * block
    targets = n_ab * n_cd
    piece = group * group
    own_place = me_ab * n_cd + me_cd

    tile_copies = [
        pltpu.make_async_copy(tiles_ref.at[k], tiles.at[k], tile_sem.at[k]) for k in range(slots)
    ]
    for copy in tile_copies:
        copy.start()
    own = pltpu.make_async_copy(amp_ref, gathered.at[0], own_sem)
    own.start()

    barrier = pltpu.get_barrier_semaphore()
    for j in range(1, n_ab):
        pl.semaphore_signal(
            barrier, inc=1, device_id=(lax.rem(me_ab + j, n_ab), me_cd, me_ij), device_id_type=MESH
        )
    pl.semaphore_signal(barrier, inc=1, device_id=(me_ab, me_cd, 1 - me_ij), device_id_type=MESH)

    @pl.when(me_cd > 0)
    def _():
        pl.semaphore_signal(barrier, inc=1, device_id=(me_ab, me_cd - 1, me_ij), device_id_type=MESH)

    @pl.when(me_cd < n_cd - 1)
    def _():
        pl.semaphore_signal(barrier, inc=1, device_id=(me_ab, me_cd + 1, me_ij), device_id_type=MESH)

    ends = jnp.where(me_cd > 0, 1, 0) + jnp.where(me_cd < n_cd - 1, 1, 0)
    pl.semaphore_wait(barrier, n_ab + ends)

    ag = {}
    for h in range(chunks):
        part = pl.ds(h * LANES, LANES)
        for j in range(1, n_ab):
            ag[h, j] = pltpu.make_async_remote_copy(
                src_ref=amp_ref.at[part],
                dst_ref=gathered.at[j, part],
                send_sem=ag_send.at[h, j],
                recv_sem=ag_recv.at[h, j],
                device_id=(lax.rem(me_ab + j, n_ab), me_cd, me_ij),
                device_id_type=MESH,
            )
            if h == 0:
                ag[h, j].start()

    keys = [row_ref[k] * n_ab + col_ref[k] for k in range(slots)]
    live_count = count_ref[0]
    for copy in tile_copies:
        copy.wait()
    for j in range(n_ab):
        column = lax.rem(me_ab - j + n_ab, n_ab)
        for r in range(n_ab):
            slot = jnp.int32(0)
            for k in range(1, slots):
                slot = jnp.where(keys[k] == r * n_ab + column, jnp.int32(k), slot)
            scale = jnp.where(slot < live_count, jnp.float32(1), jnp.float32(0))
            high, low = split(tiles[slot] * scale)
            at = (slice(None), pl.ds(r * block, block), pl.ds(j * size, size))
            w_high[at] = high.reshape(block, block, size)
            w_low[at] = low.reshape(block, block, size)

    own.wait()
    mi = {}
    contract = (((1,), (1,)), ((), ()))
    last = n_cd - 1

    def up(h, d, source):
        return pltpu.make_async_remote_copy(
            src_ref=source.at[h, d],
            dst_ref=up_in.at[h, d],
            send_sem=up_send.at[h, d],
            recv_sem=up_recv.at[h, d],
            device_id=(me_ab, me_cd + 1, me_ij),
            device_id_type=MESH,
        )

    def down(h, d, source):
        return pltpu.make_async_remote_copy(
            src_ref=source.at[h, d],
            dst_ref=down_in.at[h, d],
            send_sem=down_send.at[h, d],
            recv_sem=down_recv.at[h, d],
            device_id=(me_ab, me_cd - 1, me_ij),
            device_id_type=MESH,
        )

    def compute(h):
        part = pl.ds(h * LANES, LANES)
        for j in range(n_ab):
            if j:
                ag[h, j].wait_recv()
                if h + 1 < chunks:
                    ag[h + 1, j].start()
            high, low = split(gathered[j, part])
            a_both[pl.ds(0, LANES), pl.ds(j * size, size)] = high
            a_both[pl.ds(LANES, LANES), pl.ds(j * size, size)] = low
        for i in range(n_cd):
            d = jnp.where(me_cd < n_cd // 2, last - i, i)
            lead = pl.ds(d * group, group)
            left_high = w_high[lead].reshape(rows, n_ab * size)
            left_low = w_low[lead].reshape(rows, n_ab * size)
            right = a_both[...]
            wide = lax.dot_general(left_high, right, contract, preferred_element_type=jnp.float32)
            value = wide[:, LANES:] + lax.dot_general(
                left_low, right[:LANES], contract, preferred_element_type=jnp.float32
            )
            value += wide[:, :LANES]
            partial[h, d] = value
            if i < last:

                @pl.when(me_cd == 0)
                def _():
                    up(h, d, partial).start()

                @pl.when(me_cd == last)
                def _():
                    down(h, d, partial).start()

    def relay(h, step):
        for_up = last + me_cd - step

        @pl.when((me_cd >= 1) & (me_cd <= step))
        def _():
            up(h, for_up, up_out).wait_recv()
            if step < last:
                up_out[h, for_up] = partial[h, for_up] + up_in[h, for_up]
                up(h, for_up, up_out).start()

        for_down = step - last + me_cd

        @pl.when((me_cd < last) & (for_down >= 0))
        def _():
            down(h, for_down, down_out).wait_recv()
            if step < last:
                down_out[h, for_down] = partial[h, for_down] + down_in[h, for_down]
                down(h, for_down, down_out).start()

    def finish(h):
        summed[h] = partial[h, me_cd]

        @pl.when(me_cd > 0)
        def _():
            summed[h] += up_in[h, me_cd]

        @pl.when(me_cd < last)
        def _():
            summed[h] += down_in[h, me_cd]

        for x in range(group):
            for y in range(group):
                outgoing[h, pl.ds(x * group + y, targets, stride=piece), :] = summed[
                    h, pl.ds(x * n_ab * block + y, targets, stride=group), :
                ]
        for i in range(n_cd):
            q = jnp.where(me_cd < n_cd // 2, last - i, i)
            for j in range(n_ab):
                p = lax.rem(me_ab + j, n_ab)
                t = p * n_cd + q
                mi[h, i, j] = pltpu.make_async_remote_copy(
                    src_ref=outgoing.at[h, pl.ds(t * piece, piece)],
                    dst_ref=mirrored.at[h, pl.ds(own_place * piece, piece)],
                    send_sem=mi_send.at[h, t],
                    recv_sem=mi_recv.at[h, own_place],
                    device_id=(p, q, 1 - me_ij),
                    device_id_type=MESH,
                )
                mi[h, i, j].start()

    waiting = None
    for h in range(chunks):
        compute(h)
        if waiting is not None:
            for step in range(2, n_cd):
                relay(waiting, step)
            finish(waiting)
        relay(h, 1)
        waiting = h
    for step in range(2, n_cd):
        relay(waiting, step)
    finish(waiting)
    for h in range(chunks):
        for s in range(targets):
            pltpu.make_async_remote_copy(
                src_ref=outgoing.at[h, pl.ds(s * piece, piece)],
                dst_ref=mirrored.at[h, pl.ds(s * piece, piece)],
                send_sem=mi_send.at[h, s],
                recv_sem=mi_recv.at[h, s],
                device_id=(me_ab, me_cd, 1 - me_ij),
                device_id_type=MESH,
            ).wait_recv()
        for y in range(group):
            out_ref[y, :, pl.ds(h * LANES, LANES)] = (
                summed[h, pl.ds(y * n_ab * block, n_ab * block), :]
                + mirrored[h, pl.ds(y, targets * group, stride=group), :]
            )
    for h in range(chunks):
        for d in range(n_cd):

            @pl.when(me_cd < d)
            def _():
                up(h, d, up_out).wait_send()

            @pl.when(me_cd > d)
            def _():
                down(h, d, down_out).wait_send()

    for copy in [*ag.values(), *mi.values()]:
        copy.wait_send()


def fused(amplitudes, integrals, tile_row, tile_col, tile_count):
    occ_dev = amplitudes.shape[0]
    slots, size = integrals.shape[0], integrals.shape[1]
    block = math.isqrt(size)
    n_ab, n_cd = lax.axis_size("ab"), lax.axis_size("cd")
    group = block // n_cd
    rows = group * n_ab * block
    chunks = occ_dev // LANES
    targets = n_ab * n_cd
    piece = group * group
    f32, bf16 = jnp.float32, jnp.bfloat16
    dma = pltpu.SemaphoreType.DMA
    out = pl.pallas_call(
        functools.partial(ladder_kernel, n_ab, n_cd, block, chunks),
        out_shape=jax.ShapeDtypeStruct((group, n_ab * block, occ_dev), f32),
        in_specs=[pl.BlockSpec(memory_space=pltpu.SMEM)] * 3
        + [pl.BlockSpec(memory_space=pl.ANY)] * 2,
        out_specs=pl.BlockSpec(memory_space=pltpu.VMEM),
        scratch_shapes=[
            pltpu.VMEM((slots, size, size), f32),
            pltpu.VMEM((block, n_ab * block, n_ab * size), bf16),
            pltpu.VMEM((block, n_ab * block, n_ab * size), bf16),
            pltpu.VMEM((n_ab, occ_dev, size), f32),
            pltpu.VMEM((2 * LANES, n_ab * size), bf16),
            *[pltpu.VMEM((chunks, n_cd, rows, LANES), f32)] * 5,
            pltpu.VMEM((chunks, rows, LANES), f32),
            pltpu.VMEM((chunks, targets * piece, LANES), f32),
            pltpu.VMEM((chunks, targets * piece, LANES), f32),
            dma((slots,)),
            dma,
            dma((chunks, n_ab)),
            dma((chunks, n_ab)),
            *[dma((chunks, n_cd))] * 4,
            dma((chunks, targets)),
            dma((chunks, targets)),
        ],
        compiler_params=pltpu.CompilerParams(
            collective_id=0, has_side_effects=True, vmem_limit_bytes=VMEM_BYTES
        ),
    )(tile_row, tile_col, tile_count, amplitudes, integrals)
    return jnp.transpose(out, (2, 0, 1))[:, None]


def from_partner(block, axis, bit):
    count = lax.axis_size(axis)
    route = []
    for low in range(count):
        high = low | 1 << bit
        if high != low and high < count:
            route += [(low, high), (high, low)]
    return lax.ppermute(block, axis, route)


def place_rows(chosen, tile_rows, row_picks, block_size):
    terms = jnp.einsum("okf,kef->oke", chosen, tile_rows, precision=lax.Precision.HIGHEST)
    occ_dev, slots, width = terms.shape
    terms = terms.reshape(occ_dev, slots, width // block_size, block_size)
    placed = jnp.einsum("rk,okab->aorb", row_picks, terms, precision=lax.Precision.HIGHEST)
    return placed.reshape(width // block_size, occ_dev, row_picks.shape[0] * block_size)


def general(amplitudes, integrals, tile_row, tile_col, tile_count):
    occ_dev = amplitudes.shape[0]
    slots = integrals.shape[0]
    tile_size = integrals.shape[1]
    block_size = math.isqrt(tile_size)
    blocks = lax.axis_size("ab")
    cd_size = lax.axis_size("cd")
    group_size = block_size // cd_size
    live_count = tile_count[0]
    live = jnp.arange(slots, dtype=jnp.int32) < live_count
    row_picks = (
        (tile_row[None, :] == jnp.arange(blocks, dtype=jnp.int32)[:, None]) & live[None, :]
    ).astype(jnp.float32)
    gathered = lax.all_gather(amplitudes, "ab", axis=1, tiled=True)
    columns = gathered.reshape(occ_dev, -1, tile_size)
    chosen = jnp.take(columns, tile_col, axis=1)
    partial_value = place_rows(chosen, integrals, row_picks, block_size)
    summed = lax.psum_scatter(partial_value, "cd", scatter_dimension=0, tiled=True)
    direct = jnp.transpose(summed, (1, 0, 2))
    outgoing = summed.reshape(group_size, occ_dev, blocks, cd_size, group_size)
    outgoing = jnp.transpose(outgoing, (2, 3, 1, 0, 4))
    arrived = lax.all_to_all(
        outgoing.reshape(blocks * cd_size, occ_dev * group_size * group_size),
        ("ab", "cd"),
        split_axis=0,
        concat_axis=0,
        tiled=True,
    )
    arrived = arrived.reshape(blocks, cd_size, occ_dev, group_size, group_size)
    mirrored = jnp.transpose(arrived, (2, 4, 0, 1, 3)).reshape(
        occ_dev, group_size, blocks * block_size
    )
    partner = from_partner(mirrored, "ij", 0)
    return (direct + partner).reshape(occ_dev, 1, group_size, blocks * block_size)


def per_device(amplitudes, integrals, tile_row, tile_col, tile_count):
    n_ab = lax.axis_size("ab")
    if (
        amplitudes.shape[1] == integrals.shape[1]
        and integrals.shape[0] == n_ab * n_ab
        and lax.axis_size("ij") == 2
        and amplitudes.shape[0] % LANES == 0
    ):
        return fused(amplitudes, integrals, tile_row, tile_col, tile_count)
    return general(amplitudes, integrals, tile_row, tile_col, tile_count)


def solution(mesh):
    in_specs = (
        P("ij", ("cd", "ab")),
        P(("ab", "cd"), None, None),
        P(("ab", "cd")),
        P(("ab", "cd")),
        P(("ab", "cd")),
    )
    out_specs = P("ij", "ab", "cd", None)
    return jax.shard_map(
        per_device, mesh=mesh, in_specs=in_specs, out_specs=out_specs, check_vma=False
    )
```
